768 devices in a mesh: row: 24 (over z, x_lo), col: 32 (over y, x_hi, core).
Axes of the slice: x: 4 (x_hi: 2, x_lo: 2; x = x_hi * 2 + x_lo), y: 8, z: 12, core: 2. Of those that a mesh axis runs over, the one named last changes fastest.
Arguments:
- densities: bfloat16 [30720, 4500], P('col'), may hold values from -0.75 to 0.75
- coupling_a: float32 [5, 900], replicated, may hold values from -6 to 6
- coupling_b: float32 [5, 900], replicated, may hold values from -6 to 6
- energies: float32 [30720], replicated, may hold values from 2 to 40
- strength: float32 [30720], replicated, may hold values from -6 to 6
- qp_index: int32 [30720, 2], replicated, may hold values from 0 to 1023
- kpi_label: int32 [30720], replicated, may hold values from 0 to 15
- amplitude_u: float32 [1024], replicated, may hold values from 0.1 to 1
- amplitude_v: float32 [1024], replicated, may hold values from 0.1 to 1
- panel_blocks: int32 [2], replicated, may hold values from 0 to 15, as said below
Outputs:
- matrix_a: float32 [2, 960, 30720], P(None, 'row', 'col')
- matrix_b: float32 [2, 960, 30720], P(None, 'row', 'col')
- response: float32 [2, 960], P(None, 'row')
- mirror: float32 [2, 30720], P(None, 'col')
The draws below stay inside these ranges and needn't reach their ends.
Inputs may be any that keep to these rules, and one draw needn't show every extreme that they name: `panel_blocks`: both blocks lie in the lower half of the column blocks, one of them is block 15, and the two may coincide.
All inputs are finite; a program needn't handle non-finite values.
Results may differ from the reference program's by a relative error of at most 0.007.
Values may be sent and summed in bfloat16 or wider, within the bound.
A program may use at most 64 MiB of HBM per device.

```python
import math
import jax
import jax.numpy as jnp
from jax import lax

POINTS = 900
TYPES = 5
NQP = 1024
NKPI = 16
COLB = 960
NBLK = 32
NPAIRS = 30720


def draw_panel_blocks(key, part):
    first_key = jax.random.fold_in(key, 7001)
    second_key = jax.random.fold_in(key, 7002)
    top_block = NBLK // 2 - 1
    other = jax.random.randint(first_key, (), 0, NBLK // 2, dtype=jnp.int32)
    flipped = jax.random.randint(second_key, (), 0, 2, dtype=jnp.int32)
    top_value = jnp.full((), top_block, dtype=jnp.int32)
    return jnp.where(flipped == 0, jnp.stack([top_value, other]), jnp.stack([other, top_value])).astype(jnp.int32)


def with_ends(drawn, own_key, low, high):
    longest = drawn.shape.index(max(drawn.shape))
    spots = []
    for shift in (0, 1):
        where = [jax.random.randint(jax.random.fold_in(own_key, axis), (), 0, length) for axis, length in enumerate(drawn.shape)]
        where[longest] = (where[longest] + shift) % drawn.shape[longest]
        spots.append(tuple(where))
    return drawn.at[spots[0]].set(low).at[spots[1]].set(high)


def levels(stream_key, dims, pieces, smallest, high):
    level, own = 1.0, jax.random.fold_in(stream_key, 6)
    for dim, shards_of in pieces:
        steps = jnp.exp(jax.random.uniform(jax.random.fold_in(own, dim), (shards_of,), jnp.float32, smallest / len(pieces), high / len(pieces)))
        level = level * jnp.repeat(steps, dims[dim] // shards_of).reshape([-1 if axis == dim else 1 for axis in range(len(dims))])
    return level


def noise(key, extent, scale, most, split=(), kind=jnp.bfloat16):
    result = scale * jax.random.normal(key, extent, jnp.float32)
    if split:
        result = result * levels(key, extent, split, -0.22, 0.18)
    return jnp.clip(result, -most, most).astype(kind)


def setup_inputs(seed: int = 0) -> dict:
    arg_keys = jax.random.split(jax.random.key(seed), 11)
    return {
        "densities": noise(arg_keys[0], (NPAIRS, TYPES * POINTS), 0.12, 0.75, ((0, 32),)),
        "coupling_a": noise(arg_keys[1], (TYPES, POINTS), 1.0, 6.0, (), jnp.float32),
        "coupling_b": noise(arg_keys[2], (TYPES, POINTS), 1.0, 6.0, (), jnp.float32),
        "energies": jnp.clip(jnp.exp(jax.random.uniform(arg_keys[3], (NPAIRS,), jnp.float32, math.log(2.0), math.log(40.0))), 2.0, 40.0),
        "strength": noise(arg_keys[4], (NPAIRS,), 1.0, 6.0, (), jnp.float32),
        "qp_index": with_ends(jax.random.randint(arg_keys[5], (NPAIRS, 2), 0, NQP), jax.random.fold_in(arg_keys[5], 1), 0, NQP - 1).astype(jnp.int32),
        "kpi_label": with_ends(jax.random.randint(arg_keys[6], (NPAIRS,), 0, NKPI), jax.random.fold_in(arg_keys[6], 1), 0, NKPI - 1).astype(jnp.int32),
        "amplitude_u": jnp.clip(jax.random.uniform(arg_keys[7], (NQP,), jnp.float32, 0.1, 1.0), 0.1, 1.0),
        "amplitude_v": jnp.clip(jax.random.uniform(arg_keys[8], (NQP,), jnp.float32, 0.1, 1.0), 0.1, 1.0),
        "panel_blocks": draw_panel_blocks(jax.random.fold_in(arg_keys[10], 71), 0),
    }


PAIRING = 1.0
HIGH = lax.Precision.HIGHEST

def pair_factors(qp_part, label_part, amplitude_u, amplitude_v):
    states = lax.broadcasted_iota(jnp.int32, (1, amplitude_u.shape[0]), 1)
    amp_table = jnp.stack([amplitude_u, amplitude_v], axis=1)
    first_amp = jnp.dot((qp_part[:, 0:1] == states).astype(jnp.float32), amp_table, precision=HIGH)
    second_amp = jnp.dot((qp_part[:, 1:2] == states).astype(jnp.float32), amp_table, precision=HIGH)
    anomal = first_amp[:, 0] * second_amp[:, 1] + first_amp[:, 1] * second_amp[:, 0]
    direct = first_amp[:, 0] * second_amp[:, 0] - first_amp[:, 1] * second_amp[:, 1]
    labels = lax.broadcasted_iota(jnp.int32, (1, NKPI), 1)
    member = (label_part[:, None] == labels).astype(jnp.float32)
    return (anomal, direct, member)

def reference(densities, coupling_a, coupling_b, energies, strength, qp_index, kpi_label, amplitude_u, amplitude_v, panel_blocks):
    total_pairs = densities.shape[0]
    weight_a = coupling_a.reshape(-1)
    weight_b = coupling_b.reshape(-1)
    anomal, direct, member = pair_factors(qp_index, kpi_label, amplitude_u, amplitude_v)
    col_global = jnp.arange(total_pairs, dtype=jnp.int32)
    col_block = col_global // COLB
    list_a, list_b, list_resp, list_mirror = ([], [], [], [])
    for which in range(2):
        block_id = panel_blocks[which].astype(jnp.int32)
        start = (block_id * COLB).astype(jnp.int32)
        panel = lax.dynamic_slice_in_dim(densities, start, COLB, 0)
        weighted = jnp.concatenate([(panel.astype(jnp.float32) * weight_a).astype(jnp.bfloat16), (panel.astype(jnp.float32) * weight_b).astype(jnp.bfloat16)], 0)
        product = lax.dot_general(weighted, densities, (((1,), (1,)), ((), ())), preferred_element_type=jnp.float32)
        row_anomal = lax.dynamic_slice_in_dim(anomal, start, COLB, 0)
        row_direct = lax.dynamic_slice_in_dim(direct, start, COLB, 0)
        row_member = lax.dynamic_slice_in_dim(member, start, COLB, 0)
        row_energy = lax.dynamic_slice_in_dim(energies, start, COLB, 0)
        row_strength = lax.dynamic_slice_in_dim(strength, start, COLB, 0)
        pair_a = jnp.dot(row_anomal[:, None] * row_member, (anomal[:, None] * member).T, precision=HIGH)
        pair_b = jnp.dot(row_direct[:, None] * row_member, (direct[:, None] * member).T, precision=HIGH)
        row_global = start + jnp.arange(COLB, dtype=jnp.int32)
        diagonal = jnp.where(row_global[:, None] == col_global[None, :], row_energy[:, None], 0.0)
        active = (col_block >= block_id)[None, :]
        mat_a = jnp.where(active, product[:COLB] + diagonal + PAIRING * pair_a, 0.0)
        mat_b = jnp.where(active, product[COLB:] + PAIRING * pair_b, 0.0)
        summed = mat_a + mat_b
        list_resp.append(jnp.dot(summed, strength, precision=HIGH) / math.sqrt(total_pairs))
        list_mirror.append(jnp.dot(row_strength, summed, precision=HIGH) / math.sqrt(COLB))
        list_a.append(mat_a)
        list_b.append(mat_b)
    return (jnp.stack(list_a), jnp.stack(list_b), jnp.stack(list_resp), jnp.stack(list_mirror))
```

```python
import functools
import math

import jax
import jax.numpy as jnp
from jax import lax
from jax.experimental import pallas as pl
from jax.experimental.pallas import tpu as pltpu
from jax.sharding import PartitionSpec as P

PAIRING = 1.0
TOP = 15
UPPER = 4
CHUNKS = 5
MESH_ID = pl.DeviceIdType.MESH


def both(*conds):
    out = conds[0]
    for cond in conds[1:]:
        out = jnp.logical_and(out, cond)
    return out


def spread_kernel(block, dens, out, buf, recv_sem, send_sem, local_sem):
    row = lax.axis_index("row")
    col = lax.axis_index("col")
    other = row + 1 - 2 * lax.rem(row, 2)
    level = col // 4
    half = lax.rem(col // 2, 2)
    core = lax.rem(col, 2)
    row_len = buf.shape[1]
    size = row_len // CHUNKS

    src_level, src_half, src_core = block // 4, (block // 2) % 2, block % 2
    here = (src_level, src_half, src_core)

    top_src = col == TOP
    top_recv = level >= UPPER
    from_src = jnp.logical_and(level == UPPER, core == 1)
    top_from_row = jnp.where(jnp.logical_and(from_src, half == 0), other, row)
    top_from_col = jnp.where(core == 0, col + 1, jnp.where(from_src, TOP, col - 4))
    top_up = both(core == 1, level >= UPPER, level < 7)
    top_mate = both(core == 1, level >= UPPER)

    same = block == TOP
    src = col == block
    root_col = src_level * 4 + (1 - src_half) * 2
    root = col == root_col
    up_dst = both(level > src_level, level < UPPER)
    relay_zero = jnp.logical_and(src_level == 3, both(level == 0, core == 0))
    root_needs = jnp.logical_and(col > block, level == src_level)
    recv = jnp.logical_or(jnp.logical_or(col > block, root), relay_zero)
    if same:
        recv = col < 0
        src = col < 0
        root = col < 0
    src_dev = jnp.where(half == src_half, block, root_col)
    on_mate = jnp.logical_and(core == 1, col > block)
    if src_level == 3:
        entry_up = col < 0
        entry_down = both(level == 0, core == 0)
        from_zero = both(level == 7, core == 0)
    else:
        entry_up = both(level == src_level + 1, core == 0)
        entry_down = both(level == 7, core == 0)
        from_zero = col < 0
    from_col = jnp.where(
        root,
        block,
        jnp.where(
            on_mate,
            col - 1,
            jnp.where(
                jnp.logical_or(entry_up, entry_down),
                src_dev,
                jnp.where(from_zero, half * 2, jnp.where(level >= UPPER, col + 4, col - 4)),
            ),
        ),
    )
    from_row = jnp.where(root, other, row)
    start = jnp.logical_or(src, root)
    down_entry_col = (0 if src_level == 3 else 28) + half * 2
    none = col < 0
    if same:
        sends = []
        root_send = none
    else:
        up_relay = both(core == 0, level > src_level, level < 3)
        start_up = start if src_level < 3 else none
        up = jnp.logical_or(start_up, up_relay)
        up_col = jnp.where(start, (src_level + 1) * 4 + half * 2, col + 4)
        down_relay = both(core == 0, level > UPPER)
        zero_relay = both(core == 0, level == 0) if src_level == 3 else none
        down = jnp.logical_or(jnp.logical_or(start, down_relay), zero_relay)
        down_col = jnp.where(start, down_entry_col, jnp.where(zero_relay, 28 + half * 2, col - 4))
        mate = jnp.logical_and(core == 0, col >= block)
        sends = [(up, up_col), (down, down_col), (mate, col + 1)]
        root_send = src

    barrier = pltpu.get_barrier_semaphore()

    @pl.when(top_recv)
    def _():
        pl.semaphore_signal(barrier, 1, device_id=(top_from_row, top_from_col), device_id_type=MESH_ID)

    @pl.when(recv)
    def _():
        pl.semaphore_signal(barrier, 1, device_id=(from_row, from_col), device_id_type=MESH_ID)

    one = lambda cond: jnp.where(cond, 1, 0)
    count = 2 * one(top_src) + one(top_up) + one(top_mate) + one(root_send)
    for cond, _ in sends:
        count = count + one(cond)

    @pl.when(count > 0)
    def _():
        pl.semaphore_wait(barrier, count)

    def part(j):
        return pl.ds(j * size, size)

    def copy(which, slot, j, src_ref, to_row, to_col):
        return pltpu.make_async_remote_copy(
            src_ref=src_ref,
            dst_ref=buf.at[which, part(j)],
            send_sem=send_sem.at[which, slot, j],
            recv_sem=recv_sem.at[which, j],
            device_id=(to_row, to_col),
            device_id_type=MESH_ID,
        )

    def own(r, j):
        return dens.at[pl.ds(pl.multiple_of(r * row_len + j * size, 8), size)]

    def held(which, j):
        return buf.at[which, part(j)]

    def keep(which):
        return pltpu.make_async_copy(
            dens.at[pl.ds(pl.multiple_of(row * row_len, 8), row_len)], buf.at[which], local_sem.at[which]
        )

    for j in range(CHUNKS):

        @pl.when(top_src)
        def _():
            copy(0, 0, j, own(row, j), row, UPPER * 4 + 3).start()
            copy(0, 1, j, own(other, j), other, UPPER * 4 + 1).start()

        @pl.when(src)
        def _():
            for slot, (cond, to_col) in enumerate(sends):

                @pl.when(cond)
                def _():
                    copy(1, slot, j, own(row, j), row, to_col).start()

            copy(1, 3, j, own(other, j), other, root_col).start()

    @pl.when(top_src)
    def _():
        keep(0).start()

    @pl.when(src)
    def _():
        keep(1).start()

    relay_one = jnp.logical_and(recv, core == 0)
    for j in range(CHUNKS):
        if not same:

            @pl.when(relay_one)
            def _():
                copy(1, 0, j, held(1, j), row, col).wait_recv()
                for slot, (cond, to_col) in enumerate(sends):

                    @pl.when(cond)
                    def _():
                        copy(1, slot, j, held(1, j), row, to_col).start()

        @pl.when(top_mate)
        def _():
            copy(0, 0, j, held(0, j), row, col).wait_recv()
            copy(0, 0, j, held(0, j), row, col - 1).start()

            @pl.when(top_up)
            def _():
                copy(0, 1, j, held(0, j), row, col + 4).start()

    for j in range(CHUNKS):

        @pl.when(both(top_recv, core == 0))
        def _():
            copy(0, 0, j, held(0, j), row, col).wait_recv()

        if not same:

            @pl.when(jnp.logical_and(recv, core == 1))
            def _():
                copy(1, 0, j, held(1, j), row, col).wait_recv()

    @pl.when(top_src)
    def _():
        keep(0).wait()

    @pl.when(src)
    def _():
        keep(1).wait()

    write = pltpu.make_async_copy(buf, out, local_sem.at[2])
    write.start()

    for j in range(CHUNKS):

        @pl.when(top_src)
        def _():
            copy(0, 0, j, held(0, j), row, col).wait_send()
            copy(0, 1, j, held(0, j), row, col).wait_send()

        @pl.when(top_mate)
        def _():
            copy(0, 0, j, held(0, j), row, col).wait_send()

        @pl.when(top_up)
        def _():
            copy(0, 1, j, held(0, j), row, col).wait_send()

        if not same:
            for slot, (cond, _) in enumerate(sends):

                @pl.when(cond)
                def _():
                    copy(1, slot, j, held(1, j), row, col).wait_send()

            @pl.when(src)
            def _():
                copy(1, 3, j, held(1, j), row, col).wait_send()

    write.wait()


def spread(block, row_len, dens):
    features = dens.shape[1]
    return pl.pallas_call(
        functools.partial(spread_kernel, block),
        name=f"spread_{block}",
        out_shape=jax.ShapeDtypeStruct((2, row_len, features), dens.dtype),
        in_specs=[pl.BlockSpec(memory_space=pl.ANY)],
        out_specs=pl.BlockSpec(memory_space=pl.ANY),
        scratch_shapes=[
            pltpu.VMEM((2, row_len, features), dens.dtype),
            pltpu.SemaphoreType.DMA((2, CHUNKS)),
            pltpu.SemaphoreType.DMA((2, 4, CHUNKS)),
            pltpu.SemaphoreType.DMA((3,)),
        ],
        compiler_params=pltpu.CompilerParams(collective_id=block, has_side_effects=True),
    )(dens)


def split3(x):
    hi = x.astype(jnp.bfloat16)
    rest = x - hi.astype(jnp.float32)
    mid = rest.astype(jnp.bfloat16)
    low = (rest - mid.astype(jnp.float32)).astype(jnp.bfloat16)
    return hi, mid, low


def dot_t(a, b):
    return lax.dot_general(a, b, (((1,), (1,)), ((), ())), preferred_element_type=jnp.float32)


def pick(table, index):
    states = table.shape[1]
    hit = lax.broadcasted_iota(jnp.int32, (states, index.shape[1]), 0) == index
    hit = jnp.where(hit, 1.0, 0.0).astype(jnp.bfloat16)
    parts = jnp.dot(table, hit, preferred_element_type=jnp.float32)
    u = parts[0:1] + parts[1:2] + parts[2:3]
    v = parts[3:4] + parts[4:5] + parts[5:6]
    return u, v


def compute_kernel(
    blocks,
    panels,
    dens,
    coup_a,
    coup_b,
    energies,
    strength,
    qp,
    label,
    amp_u,
    amp_v,
    mat_a,
    mat_b,
    resp_part,
    mir_part,
    weight,
    acc,
):
    row = lax.axis_index("row")
    col = lax.axis_index("col")
    row_len = panels.shape[1]
    block_len = dens.shape[0]
    features = dens.shape[1]

    types, points = coup_a.shape
    for t in range(types):
        weight[0:1, t * points : (t + 1) * points] = coup_a[t : t + 1, :]
        weight[1:2, t * points : (t + 1) * points] = coup_b[t : t + 1, :]

    slot = [jnp.where(blocks[k] == TOP, 0, 1) for k in range(2)]

    step = 512
    acc[...] = jnp.zeros_like(acc)

    def product(lo, size):
        at = pl.ds(lo, size)
        wa = weight[0:1, at]
        wb = weight[1:2, at]
        stack = []
        for k in range(2):
            p = panels[slot[k], :, at].astype(jnp.float32)
            stack += [p * wa, p * wb]
        weighted = jnp.concatenate(stack, 0).astype(jnp.bfloat16)
        acc[...] += dot_t(weighted, dens[:, at])

    def body(i, _):
        product(pl.multiple_of(i * step, step), step)
        return 0

    full = features // step
    lax.fori_loop(0, full, body, 0)
    product(full * step, features - full * step)

    odd = lax.rem(col, 2) == 1
    base = pl.multiple_of(col * block_len - jnp.where(odd, 64, 0), 128)
    wide = pl.ds(base, block_len + 64)

    def own(ref):
        x = ref[:, wide]
        return jnp.where(odd, x[:, 64:], x[:, :block_len])

    table = jnp.concatenate(
        [t.astype(jnp.float32) for t in (*split3(amp_u[...]), *split3(amp_v[...]))] + [jnp.zeros((2, amp_u.shape[1]), jnp.float32)], 0
    ).astype(jnp.bfloat16)

    def factors(pairs):
        u_i, v_i = pick(table, pairs[0:1])
        u_j, v_j = pick(table, pairs[1:2])
        return u_i * v_j + v_i * u_j, u_i * u_j - v_i * v_j

    col_anomal, col_direct = factors(own(qp))
    col_label = own(label)
    col_strength = own(strength)
    col_global = col * block_len + lax.broadcasted_iota(jnp.int32, (1, block_len), 1)

    sums = []
    for k in range(2):
        first = blocks[k] * block_len + row * row_len
        near = pl.multiple_of(first // 128 * 128, 128)
        shift = first - near

        def rows_of(ref):
            x = pltpu.roll(ref[:, pl.ds(near, 256)], 256 - shift, axis=1)
            return x[:, :128]

        row_anomal, row_direct = factors(rows_of(qp))
        packed = jnp.concatenate(
            [
                row_anomal,
                row_direct,
                rows_of(label).astype(jnp.float32),
                rows_of(energies),
                rows_of(strength),
                jnp.zeros((3, 128), jnp.float32),
            ],
            0,
        )
        tall = packed.T[:row_len]
        anomal, direct, lab, energy, stren = (tall[:, i : i + 1] for i in range(5))
        row_global = first + lax.broadcasted_iota(jnp.int32, (row_len, 1), 0)
        active = col >= blocks[k]
        agree = lab == col_label.astype(jnp.float32)
        prod_a = acc[2 * k * row_len : (2 * k + 1) * row_len]
        prod_b = acc[(2 * k + 1) * row_len : (2 * k + 2) * row_len]
        a = prod_a + jnp.where(row_global == col_global, energy, 0.0)
        a = a + PAIRING * jnp.where(agree, anomal * col_anomal, 0.0)
        b = prod_b + PAIRING * jnp.where(agree, direct * col_direct, 0.0)
        a = jnp.where(active, a, 0.0)
        b = jnp.where(active, b, 0.0)
        mat_a[k] = a
        mat_b[k] = b
        both_ab = a + b
        sums.append(both_ab)
        mir_part[k : k + 1, :] = jnp.sum(both_ab * stren, axis=0, keepdims=True)
    summed = jnp.concatenate(sums, 0)
    resp = jnp.sum(summed * col_strength, axis=1, keepdims=True)
    wide_resp = jnp.concatenate([resp, jnp.zeros((128 - 2 * row_len, 1), jnp.float32)], 0)
    wide_resp = jnp.broadcast_to(wide_resp, (128, 8 * 16)).T
    resp_part[...] = wide_resp[0:1]


def reduce_kernel(
    resp_in,
    mir_in,
    response,
    mirror,
    resp_all,
    mir_pair,
    mir_all,
    resp_send,
    resp_recv,
    pair_send,
    pair_recv,
    mir_send,
    mir_recv,
):
    row = lax.axis_index("row")
    col = lax.axis_index("col")
    rows = lax.axis_size("row")
    cols = lax.axis_size("col")
    other = row + 1 - 2 * lax.rem(row, 2)
    deep = rows // 2
    z = row // 2
    row_len = response.shape[1]
    block_len = mirror.shape[1]
    total = block_len * cols

    barrier = pltpu.get_barrier_semaphore()

    def greet_col(d, _):
        pl.semaphore_signal(barrier, 1, device_id=(row, lax.rem(col + d, cols)), device_id_type=MESH_ID)
        return 0

    def greet_deep(d, _):
        to = lax.rem(z + d, deep) * 2 + lax.rem(row, 2)
        pl.semaphore_signal(barrier, 1, device_id=(to, col), device_id_type=MESH_ID)
        return 0

    lax.fori_loop(1, cols, greet_col, 0)
    lax.fori_loop(1, deep, greet_deep, 0)
    pl.semaphore_signal(barrier, 1, device_id=(other, col), device_id_type=MESH_ID)

    resp_all[col] = resp_in[...]
    mir_pair[0] = mir_in[...]
    pl.semaphore_wait(barrier, cols - 1 + deep - 1 + 1)

    def send_resp(d, _):
        pltpu.make_async_remote_copy(
            src_ref=resp_all.at[col],
            dst_ref=resp_all.at[col],
            send_sem=resp_send,
            recv_sem=resp_recv,
            device_id=(row, lax.rem(col + d, cols)),
            device_id_type=MESH_ID,
        ).start()
        return 0

    pair = pltpu.make_async_remote_copy(
        src_ref=mir_pair.at[0],
        dst_ref=mir_pair.at[1],
        send_sem=pair_send,
        recv_sem=pair_recv,
        device_id=(other, col),
        device_id_type=MESH_ID,
    )
    pair.start()
    lax.fori_loop(1, cols, send_resp, 0)
    pair.wait_recv()
    mir_all[z] = mir_pair[0] + mir_pair[1]

    def send_mir(d, _):
        to = lax.rem(z + d, deep) * 2 + lax.rem(row, 2)
        pltpu.make_async_remote_copy(
            src_ref=mir_all.at[z],
            dst_ref=mir_all.at[z],
            send_sem=mir_send,
            recv_sem=mir_recv,
            device_id=(to, col),
            device_id_type=MESH_ID,
        ).start()
        return 0

    lax.fori_loop(1, deep, send_mir, 0)

    def wait_all(ref, count, sem):
        some = ref.at[pl.ds(0, count)]
        pltpu.make_async_copy(some, some, sem).wait()

    wait_all(resp_all, cols - 1, resp_recv)
    r = jnp.sum(resp_all[...], axis=0) * (1.0 / math.sqrt(total))
    response[0:1, :] = r[:, :row_len]
    response[1:2, :] = r[:, row_len : 2 * row_len]
    wait_all(mir_all, deep - 1, mir_recv)
    m = jnp.sum(mir_all[...], axis=0) * (1.0 / math.sqrt(block_len))
    mirror[...] = m
    wait_all(resp_all, cols - 1, resp_send)
    wait_all(mir_all, deep - 1, mir_send)
    pair.wait_send()


def compute(panels, dens, coup_a, coup_b, energies, strength, qp, label, amp_u, amp_v, blocks):
    row_len, features = panels.shape[1:]
    block_len = dens.shape[0]
    vmem = pl.BlockSpec(memory_space=pltpu.VMEM)
    out = jax.ShapeDtypeStruct
    f32 = jnp.float32
    return pl.pallas_call(
        compute_kernel,
        name="compute",
        out_shape=(
            out((2, row_len, block_len), f32),
            out((2, row_len, block_len), f32),
            out((1, 128), f32),
            out((2, block_len), f32),
        ),
        in_specs=[pl.BlockSpec(memory_space=pltpu.SMEM)] + [vmem] * 10,
        out_specs=(vmem,) * 4,
        scratch_shapes=[
            pltpu.VMEM((8, features), f32),
            pltpu.VMEM((4 * row_len, block_len), f32),
        ],
        compiler_params=pltpu.CompilerParams(vmem_limit_bytes=24 * 1024 * 1024),
    )(blocks, panels, dens, coup_a, coup_b, energies, strength, qp, label, amp_u, amp_v)


def reduce(rows, cols, row_len, resp_part, mir_part):
    block_len = mir_part.shape[1]
    vmem = pl.BlockSpec(memory_space=pltpu.VMEM)
    out = jax.ShapeDtypeStruct
    f32 = jnp.float32
    return pl.pallas_call(
        reduce_kernel,
        name="reduce",
        out_shape=(out((2, row_len), f32), out((2, block_len), f32)),
        in_specs=[vmem, vmem],
        out_specs=(vmem, vmem),
        scratch_shapes=[
            pltpu.VMEM((cols, 1, 128), f32),
            pltpu.VMEM((2, 2, block_len), f32),
            pltpu.VMEM((rows // 2, 2, block_len), f32),
        ]
        + [pltpu.SemaphoreType.DMA] * 6,
        compiler_params=pltpu.CompilerParams(collective_id=TOP + 1, has_side_effects=True),
    )(resp_part, mir_part)


def on_device(
    densities, coupling_a, coupling_b, energies, strength, qp_index, kpi_label, amplitude_u, amplitude_v, panel_blocks
):
    rows = lax.axis_size("row")
    cols = lax.axis_size("col")
    row_len = densities.shape[0] // rows
    moving = panel_blocks[0] + panel_blocks[1] - TOP
    branches = [functools.partial(spread, block, row_len) for block in range(TOP + 1)]
    panels = lax.switch(moving, branches, densities)
    flat = lambda x: x.reshape(1, -1)
    a, b, resp_part, mir_part = compute(
        panels,
        densities,
        coupling_a,
        coupling_b,
        flat(energies),
        flat(strength),
        qp_index.T,
        flat(kpi_label),
        flat(amplitude_u),
        flat(amplitude_v),
        panel_blocks,
    )
    response, mirror = reduce(rows, cols, row_len, resp_part, mir_part)
    return a, b, response, mirror


def solution(mesh):
    placed = (P("col", None), P(), P(), P(), P(), P(), P(), P(), P(), P())
    return jax.shard_map(
        on_device,
        mesh=mesh,
        in_specs=placed,
        out_specs=(P(None, "row", "col"), P(None, "row", "col"), P(None, "row"), P(None, "col")),
        check_vma=False,
    )
```

```python
import functools
import math

import jax
import jax.numpy as jnp
from jax import lax
from jax.experimental import pallas as pl
from jax.experimental.pallas import tpu as pltpu
from jax.sharding import PartitionSpec as P

PAIRING = 1.0
TOP = 15
UPPER = 4
STEP = 256
MESH_ID = pl.DeviceIdType.MESH


def both(*conds):
    out = conds[0]
    for cond in conds[1:]:
        out = jnp.logical_and(out, cond)
    return out


def spread_kernel(block, dens, out, buf, rows_in, pieces, recv_sem, send_sem, local_sem):
    row = lax.axis_index("row")
    col = lax.axis_index("col")
    other = row + 1 - 2 * lax.rem(row, 2)
    level = col // 4
    half = lax.rem(col // 2, 2)
    core = lax.rem(col, 2)
    count, row_len, step = buf.shape[1:]
    features = dens.shape[1]

    src_level, src_half, src_core = block // 4, (block // 2) % 2, block % 2
    here = (src_level, src_half, src_core)

    top_src = col == TOP
    top_recv = level >= UPPER
    from_src = jnp.logical_and(level == UPPER, core == 1)
    top_from_row = jnp.where(jnp.logical_and(from_src, half == 0), other, row)
    top_from_col = jnp.where(core == 0, col + 1, jnp.where(from_src, TOP, col - 4))
    top_up = both(core == 1, level >= UPPER, level < 7)
    top_mate = both(core == 1, level >= UPPER)

    same = block == TOP
    src = col == block
    root_col = src_level * 4 + (1 - src_half) * 2
    root = col == root_col
    up_dst = both(level > src_level, level < UPPER)
    relay_zero = jnp.logical_and(src_level == 3, both(level == 0, core == 0))
    root_needs = jnp.logical_and(col > block, level == src_level)
    recv = jnp.logical_or(jnp.logical_or(col > block, root), relay_zero)
    if same:
        recv = col < 0
        src = col < 0
        root = col < 0
    src_dev = jnp.where(half == src_half, block, root_col)
    turn = 6 if src_level == 3 else UPPER
    on_mate = jnp.logical_and(core == 1, col > block)
    if src_level == 3:
        entry_up = both(level == UPPER, core == 0)
        entry_down = both(level == 0, core == 0)
        from_zero = both(level == 7, core == 0)
    else:
        entry_up = both(level == src_level + 1, core == 0)
        entry_down = both(level == 7, core == 0)
        from_zero = col < 0
    from_col = jnp.where(
        root,
        block,
        jnp.where(
            on_mate,
            col - 1,
            jnp.where(
                jnp.logical_or(entry_up, entry_down),
                src_dev,
                jnp.where(from_zero, half * 2, jnp.where(level >= turn, col + 4, col - 4)),
            ),
        ),
    )
    from_row = jnp.where(root, other, row)
    start = jnp.logical_or(src, root)
    down_entry_col = (0 if src_level == 3 else 28) + half * 2
    none = col < 0
    if same:
        sends = []
        root_send = none
    else:
        up_relay = both(core == 0, level > src_level, level < turn - 1)
        up = jnp.logical_or(start, up_relay)
        up_col = jnp.where(start, (src_level + 1) * 4 + half * 2, col + 4)
        down_relay = both(core == 0, level > turn)
        zero_relay = both(core == 0, level == 0) if src_level == 3 else none
        down = jnp.logical_or(jnp.logical_or(start, down_relay), zero_relay)
        down_col = jnp.where(start, down_entry_col, jnp.where(zero_relay, 28 + half * 2, col - 4))
        mate = jnp.logical_and(core == 0, col >= block)
        sends = [(up, up_col), (down, down_col), (mate, col + 1)]
        root_send = src

    barrier = pltpu.get_barrier_semaphore()

    @pl.when(top_recv)
    def _():
        pl.semaphore_signal(barrier, 1, device_id=(top_from_row, top_from_col), device_id_type=MESH_ID)

    @pl.when(recv)
    def _():
        pl.semaphore_signal(barrier, 1, device_id=(from_row, from_col), device_id_type=MESH_ID)

    one = lambda cond: jnp.where(cond, 1, 0)
    total = 2 * one(top_src) + one(top_up) + one(top_mate) + one(root_send)
    for cond, _ in sends:
        total = total + one(cond)

    def copy(which, slot, j, src_ref, to_row, to_col):
        return pltpu.make_async_remote_copy(
            src_ref=src_ref,
            dst_ref=buf.at[which, j],
            send_sem=send_sem.at[which, slot, j],
            recv_sem=recv_sem.at[which, j],
            device_id=(to_row, to_col),
            device_id_type=MESH_ID,
        )

    def held(which, j):
        return buf.at[which, j]

    def each(body):
        def step_of(j, carry):
            body(j)
            return carry

        lax.fori_loop(0, count, step_of, 0)

    any_src = jnp.logical_or(top_src, src)

    def load(k, r):
        rows = dens.at[pl.ds(pl.multiple_of(r * row_len, 8), row_len)]
        return pltpu.make_async_copy(rows, rows_in.at[k], local_sem.at[k])

    @pl.when(any_src)
    def _():
        load(0, row).start()
        load(1, other).start()
        load(0, row).wait()
        load(1, other).wait()
        for k in range(2):
            for j in range(count):
                width = min(step, features - j * step)
                pieces[k, j, :, 0:width] = rows_in[k, :, j * step : j * step + width]

    @pl.when(total > 0)
    def _():
        pl.semaphore_wait(barrier, total)

    @pl.when(top_src)
    def _():
        def send(j):
            copy(0, 0, j, pieces.at[0, j], row, UPPER * 4 + 3).start()
            copy(0, 1, j, pieces.at[1, j], other, UPPER * 4 + 1).start()

        each(send)

    if not same:

        @pl.when(src)
        def _():
            def send(j):
                copy(1, 3, j, pieces.at[1, j], other, root_col).start()
                for slot, (cond, to_col) in enumerate(sends):

                    @pl.when(cond)
                    def _():
                        copy(1, slot, j, pieces.at[0, j], row, to_col).start()

            each(send)

    if not same:

        @pl.when(jnp.logical_and(recv, core == 0))
        def _():
            def pass_on(j):
                copy(1, 0, j, held(1, j), row, col).wait_recv()
                for slot, (cond, to_col) in enumerate(sends):

                    @pl.when(cond)
                    def _():
                        copy(1, slot, j, held(1, j), row, to_col).start()

            each(pass_on)

    @pl.when(top_mate)
    def _():
        def pass_on(j):
            copy(0, 0, j, held(0, j), row, col).wait_recv()

            @pl.when(top_up)
            def _():
                copy(0, 1, j, held(0, j), row, col + 4).start()

            copy(0, 0, j, held(0, j), row, col - 1).start()

        each(pass_on)

    @pl.when(both(top_recv, core == 0))
    def _():
        each(lambda j: copy(0, 0, j, held(0, j), row, col).wait_recv())

    if not same:

        @pl.when(jnp.logical_and(recv, core == 1))
        def _():
            each(lambda j: copy(1, 0, j, held(1, j), row, col).wait_recv())

    def write(which, ref):
        return pltpu.make_async_copy(ref, out.at[which], local_sem.at[2 + which])

    for which, mine in ((0, top_src), (1, src)):

        @pl.when(mine)
        def _():
            write(which, pieces.at[0]).start()

        @pl.when(jnp.logical_not(mine))
        def _():
            write(which, buf.at[which]).start()

    @pl.when(top_src)
    def _():
        def wait(j):
            copy(0, 0, j, held(0, j), row, col).wait_send()
            copy(0, 1, j, held(0, j), row, col).wait_send()

        each(wait)

    @pl.when(top_mate)
    def _():
        each(lambda j: copy(0, 0, j, held(0, j), row, col).wait_send())

    @pl.when(top_up)
    def _():
        each(lambda j: copy(0, 1, j, held(0, j), row, col).wait_send())

    for slot, (cond, _) in enumerate(sends):

        @pl.when(cond)
        def _():
            each(lambda j: copy(1, slot, j, held(1, j), row, col).wait_send())

    if not same:

        @pl.when(src)
        def _():
            each(lambda j: copy(1, 3, j, held(1, j), row, col).wait_send())

    for which in range(2):
        write(which, buf.at[which]).wait()


def spread(block, row_len, dens):
    features = dens.shape[1]
    count = -(-features // STEP)
    return pl.pallas_call(
        functools.partial(spread_kernel, block),
        name=f"spread_{block}",
        out_shape=jax.ShapeDtypeStruct((2, count, row_len, STEP), dens.dtype),
        in_specs=[pl.BlockSpec(memory_space=pl.ANY)],
        out_specs=pl.BlockSpec(memory_space=pl.ANY),
        scratch_shapes=[
            pltpu.VMEM((2, count, row_len, STEP), dens.dtype),
            pltpu.VMEM((2, row_len, features), dens.dtype),
            pltpu.VMEM((2, count, row_len, STEP), dens.dtype),
            pltpu.SemaphoreType.DMA((2, count)),
            pltpu.SemaphoreType.DMA((2, 4, count)),
            pltpu.SemaphoreType.DMA((4,)),
        ],
        compiler_params=pltpu.CompilerParams(
            collective_id=block, has_side_effects=True, vmem_limit_bytes=8 * 1024 * 1024
        ),
    )(dens)


def split3(x):
    hi = x.astype(jnp.bfloat16)
    rest = x - hi.astype(jnp.float32)
    mid = rest.astype(jnp.bfloat16)
    low = (rest - mid.astype(jnp.float32)).astype(jnp.bfloat16)
    return hi, mid, low


def dot_t(a, b):
    return lax.dot_general(a, b, (((1,), (1,)), ((), ())), preferred_element_type=jnp.float32)


def pick(table, index):
    states = table.shape[1]
    hit = lax.broadcasted_iota(jnp.int32, (states, index.shape[1]), 0) == index
    hit = jnp.where(hit, 1.0, 0.0).astype(jnp.bfloat16)
    parts = jnp.dot(table, hit, preferred_element_type=jnp.float32)
    u = parts[0:1] + parts[1:2] + parts[2:3]
    v = parts[3:4] + parts[4:5] + parts[5:6]
    return u, v


def prepare_kernel(blocks, _, strength, energies, qp, label, amp_u, amp_v, col_out, row_out, win_f, win_i, near_f, near_i, sem):
    row = lax.axis_index("row")
    col = lax.axis_index("col")
    block_len = col_out.shape[1]
    row_len = row_out.shape[1]
    f32 = jnp.float32
    odd = lax.rem(col, 2)
    base = pl.multiple_of(col * block_len - 64 * odd, 128)
    moving = blocks[0] + blocks[1] - TOP
    firsts = [TOP * block_len + row * row_len, moving * block_len + row * row_len]
    nears = [pl.multiple_of(first // 128 * 128, 128) for first in firsts]
    copies = []
    wide = pl.ds(base, block_len + 64)
    for i, (src, dst) in enumerate(
        [
            (strength.at[:, wide], win_f),
            (qp.at[:, wide], win_i.at[pl.ds(0, 2)]),
            (label.at[:, wide], win_i.at[pl.ds(2, 1)]),
        ]
        + [
            pair
            for k in range(2)
            for pair in (
                (strength.at[:, pl.ds(nears[k], 256)], near_f.at[k, pl.ds(0, 1)]),
                (energies.at[:, pl.ds(nears[k], 256)], near_f.at[k, pl.ds(1, 1)]),
                (qp.at[:, pl.ds(nears[k], 256)], near_i.at[k, pl.ds(0, 2)]),
                (label.at[:, pl.ds(nears[k], 256)], near_i.at[k, pl.ds(2, 1)]),
            )
        ]
    ):
        copies.append(pltpu.make_async_copy(src, dst, sem.at[i]))
        copies[-1].start()
    table = jnp.concatenate(
        [t.astype(f32) for t in (*split3(amp_u[...]), *split3(amp_v[...]))] + [jnp.zeros((2, amp_u.shape[1]), f32)], 0
    ).astype(jnp.bfloat16)

    def factors(pairs):
        u_i, v_i = pick(table, pairs[0:1])
        u_j, v_j = pick(table, pairs[1:2])
        return u_i * v_j + v_i * u_j, u_i * u_j - v_i * v_j

    for copy in copies:
        copy.wait()

    def own(x):
        return jnp.where(odd == 1, x[:, 64:], x[:, :block_len])

    whole = own(win_i[...])
    anomal, direct = factors(whole[0:2])
    col_out[0:1, :] = anomal
    col_out[1:2, :] = direct
    col_out[2:3, :] = whole[2:3].astype(f32)
    col_out[3:4, :] = own(win_f[...])
    for k in range(2):
        block = (TOP, moving)[k]
        shift = firsts[k] - nears[k]
        ints = pltpu.roll(near_i[k], 256 - shift, axis=1)[:, :128]
        floats = pltpu.roll(near_f[k], 256 - shift, axis=1)[:, :128]
        anomal, direct = factors(ints[0:2])
        lane = lax.broadcasted_iota(jnp.int32, (1, 128), 1)
        diagonal = firsts[k] + lane - col * block_len
        packed = jnp.concatenate(
            [
                anomal,
                direct,
                ints[2:3].astype(f32),
                floats[1:2],
                floats[0:1],
                diagonal.astype(f32),
                jnp.full((1, 128), jnp.where(col >= block, 1.0, 0.0), f32),
                jnp.full((1, 128), jnp.where(blocks[k] == TOP, 1.0, 0.0), f32),
            ],
            0,
        )
        row_out[k] = jnp.concatenate([packed, jnp.zeros((120, 128), f32)], 0).T[:row_len]


def prepare(block_len, row_len, blocks, panels, strength, energies, qp, label, amp_u, amp_v):
    anywhere = pl.BlockSpec(memory_space=pl.ANY)
    vmem = pl.BlockSpec(memory_space=pltpu.VMEM)
    out = jax.ShapeDtypeStruct
    return pl.pallas_call(
        prepare_kernel,
        name="prepare",
        out_shape=(out((8, block_len), jnp.float32), out((2, row_len, 128), jnp.float32)),
        in_specs=[pl.BlockSpec(memory_space=pltpu.SMEM)] + [anywhere] * 5 + [vmem] * 2,
        out_specs=(vmem, vmem),
        scratch_shapes=[
            pltpu.VMEM((1, block_len + 64), jnp.float32),
            pltpu.VMEM((4, block_len + 64), jnp.int32),
            pltpu.VMEM((2, 8, 256), jnp.float32),
            pltpu.VMEM((2, 8, 256), jnp.int32),
            pltpu.SemaphoreType.DMA((11,)),
        ],
        compiler_params=pltpu.CompilerParams(vmem_limit_bytes=16 * 1024 * 1024),
    )(blocks, panels, strength, energies, qp, label, amp_u, amp_v)


def finish_kernel(
    panels,
    dens,
    coup_a,
    coup_b,
    col_in,
    row_in,
    mat_a,
    mat_b,
    response,
    mirror,
    weight,
    acc,
    resp_all,
    mir_pair,
    mir_all,
    resp_send,
    resp_recv,
    pair_send,
    pair_recv,
    mir_send,
    mir_recv,
):
    row = lax.axis_index("row")
    col = lax.axis_index("col")
    rows = lax.axis_size("row")
    cols = lax.axis_size("col")
    other = row + 1 - 2 * lax.rem(row, 2)
    deep = rows // 2
    z = row // 2
    row_len = mat_a.shape[1]
    block_len = dens.shape[0]
    features = dens.shape[1]
    total = block_len * cols

    barrier = pltpu.get_barrier_semaphore()

    def greet_col(d, _):
        pl.semaphore_signal(barrier, 1, device_id=(row, lax.rem(col + d, cols)), device_id_type=MESH_ID)
        return 0

    def greet_deep(d, _):
        to = lax.rem(z + d, deep) * 2 + lax.rem(row, 2)
        pl.semaphore_signal(barrier, 1, device_id=(to, col), device_id_type=MESH_ID)
        return 0

    lax.fori_loop(1, cols, greet_col, 0)
    lax.fori_loop(1, deep, greet_deep, 0)
    pl.semaphore_signal(barrier, 1, device_id=(other, col), device_id_type=MESH_ID)

    types, points = coup_a.shape
    for t in range(types):
        weight[0:1, t * points : (t + 1) * points] = coup_a[t : t + 1, :]
        weight[1:2, t * points : (t + 1) * points] = coup_b[t : t + 1, :]

    acc[...] = jnp.zeros_like(acc)

    def product(j, lo, size):
        at = pl.ds(lo, size)
        wa = weight[0:1, at]
        wb = weight[1:2, at]
        stack = []
        for k in range(2):
            p = jnp.concatenate([panels[k, j], panels[k, j + 1]], 1)[:, :size].astype(jnp.float32)
            stack += [p * wa, p * wb]
        weighted = jnp.concatenate(stack, 0).astype(jnp.bfloat16)
        acc[...] += dot_t(weighted, dens[:, at])

    def body(i, carry):
        product(2 * i, pl.multiple_of(i * 2 * STEP, 2 * STEP), 2 * STEP)
        return carry

    full = features // (2 * STEP)
    lax.fori_loop(0, full, body, 0)
    product(2 * full, full * 2 * STEP, features - full * 2 * STEP)

    col_anomal = col_in[0:1, :]
    col_direct = col_in[1:2, :]
    col_label = col_in[2:3, :]
    col_strength = col_in[3:4, :]
    lane = lax.broadcasted_iota(jnp.int32, (1, block_len), 1).astype(jnp.float32)
    mats = []
    for k in range(2):
        anomal, direct, lab, energy, stren, diagonal, active, _ = (row_in[k, :, i : i + 1] for i in range(8))
        agree = lab == col_label
        prod_a = acc[2 * k * row_len : (2 * k + 1) * row_len]
        prod_b = acc[(2 * k + 1) * row_len : (2 * k + 2) * row_len]
        a = prod_a + jnp.where(diagonal == lane, energy, 0.0)
        a = a + PAIRING * jnp.where(agree, anomal * col_anomal, 0.0)
        b = prod_b + PAIRING * jnp.where(agree, direct * col_direct, 0.0)
        a = jnp.where(active > 0.0, a, 0.0)
        b = jnp.where(active > 0.0, b, 0.0)
        both_ab = a + b
        down = jnp.sum(both_ab * stren, axis=0, keepdims=True)
        across = jnp.sum(both_ab * col_strength, axis=1, keepdims=True)
        mats.append((a, b, down, across))
    resp = []
    for k in range(2):
        is_top = row_in[k, :, 7:8] > 0.0
        mat_a[k] = jnp.where(is_top, mats[0][0], mats[1][0])
        mat_b[k] = jnp.where(is_top, mats[0][1], mats[1][1])
        mir_pair[0, k : k + 1, :] = jnp.where(is_top[0:1], mats[0][2], mats[1][2])
        resp.append(jnp.where(is_top, mats[0][3], mats[1][3]))
    wide_resp = jnp.concatenate(resp + [jnp.zeros((128 - 2 * row_len, 1), jnp.float32)], 0)
    resp_all[col] = jnp.broadcast_to(wide_resp, (128, 128)).T[0:1]

    pl.semaphore_wait(barrier, cols - 1 + deep - 1 + 1)

    def send_resp(d, _):
        pltpu.make_async_remote_copy(
            src_ref=resp_all.at[col],
            dst_ref=resp_all.at[col],
            send_sem=resp_send,
            recv_sem=resp_recv,
            device_id=(row, lax.rem(col + d, cols)),
            device_id_type=MESH_ID,
        ).start()
        return 0

    pair = pltpu.make_async_remote_copy(
        src_ref=mir_pair.at[0],
        dst_ref=mir_pair.at[1],
        send_sem=pair_send,
        recv_sem=pair_recv,
        device_id=(other, col),
        device_id_type=MESH_ID,
    )
    pair.start()
    lax.fori_loop(1, cols, send_resp, 0)
    pair.wait_recv()
    mir_all[z] = (mir_pair[0] + mir_pair[1]).astype(mir_all.dtype)

    def send_mir(d, _):
        to = lax.rem(z + d, deep) * 2 + lax.rem(row, 2)
        pltpu.make_async_remote_copy(
            src_ref=mir_all.at[z],
            dst_ref=mir_all.at[z],
            send_sem=mir_send,
            recv_sem=mir_recv,
            device_id=(to, col),
            device_id_type=MESH_ID,
        ).start()
        return 0

    lax.fori_loop(1, deep, send_mir, 0)

    def wait_all(ref, count, sem):
        some = ref.at[pl.ds(0, count)]
        pltpu.make_async_copy(some, some, sem).wait()

    wait_all(resp_all, cols - 1, resp_recv)
    r = jnp.sum(resp_all[...], axis=0) * (1.0 / math.sqrt(total))
    response[0:1, :] = r[:, :row_len]
    response[1:2, :] = r[:, row_len : 2 * row_len]
    wait_all(mir_all, deep - 1, mir_recv)
    m = jnp.sum(mir_all[...].astype(jnp.float32), axis=0) * (1.0 / math.sqrt(block_len))
    mirror[...] = m
    wait_all(resp_all, cols - 1, resp_send)
    wait_all(mir_all, deep - 1, mir_send)
    pair.wait_send()


def finish(rows, cols, panels, dens, coup_a, coup_b, col_in, row_in):
    row_len = panels.shape[2]
    block_len, features = dens.shape
    vmem = pl.BlockSpec(memory_space=pltpu.VMEM)
    out = jax.ShapeDtypeStruct
    f32 = jnp.float32
    return pl.pallas_call(
        finish_kernel,
        name="finish",
        out_shape=(
            out((2, row_len, block_len), f32),
            out((2, row_len, block_len), f32),
            out((2, row_len), f32),
            out((2, block_len), f32),
        ),
        in_specs=[vmem] * 6,
        out_specs=(vmem,) * 4,
        scratch_shapes=[
            pltpu.VMEM((8, features), f32),
            pltpu.VMEM((4 * row_len, block_len), f32),
            pltpu.VMEM((cols, 1, 128), f32),
            pltpu.VMEM((2, 2, block_len), f32),
            pltpu.VMEM((rows // 2, 2, block_len), jnp.bfloat16),
        ]
        + [pltpu.SemaphoreType.DMA] * 6,
        compiler_params=pltpu.CompilerParams(
            collective_id=TOP + 1, has_side_effects=True, vmem_limit_bytes=24 * 1024 * 1024
        ),
    )(panels, dens, coup_a, coup_b, col_in, row_in)


def on_device(
    densities, coupling_a, coupling_b, energies, strength, qp_index, kpi_label, amplitude_u, amplitude_v, panel_blocks
):
    rows = lax.axis_size("row")
    cols = lax.axis_size("col")
    block_len = densities.shape[0]
    row_len = block_len // rows
    flat = lambda x: x.reshape(1, -1)
    moving = panel_blocks[0] + panel_blocks[1] - TOP
    branches = [functools.partial(spread, block, row_len) for block in range(TOP + 1)]
    panels = lax.switch(moving, branches, densities)
    col_in, row_in = prepare(
        block_len,
        row_len,
        panel_blocks,
        panels,
        flat(strength),
        flat(energies),
        qp_index.T,
        flat(kpi_label),
        flat(amplitude_u),
        flat(amplitude_v),
    )
    return finish(rows, cols, panels, densities, coupling_a, coupling_b, col_in, row_in)


def solution(mesh):
    placed = (P("col", None), P(), P(), P(), P(), P(), P(), P(), P(), P())
    return jax.shard_map(
        on_device,
        mesh=mesh,
        in_specs=placed,
        out_specs=(P(None, "row", "col"), P(None, "row", "col"), P(None, "row"), P(None, "col")),
        check_vma=False,
    )
```

```python
import functools
import math

import jax
import jax.numpy as jnp
from jax import lax
from jax.experimental import pallas as pl
from jax.experimental.pallas import tpu as pltpu
from jax.sharding import PartitionSpec as P

PAIRING = 1.0
TOP = 15
UPPER = 4
STEP = 768
MESH_ID = pl.DeviceIdType.MESH


def both(*conds):
    out = conds[0]
    for cond in conds[1:]:
        out = jnp.logical_and(out, cond)
    return out


def spread_kernel(block, dens, out, buf, rows_in, pieces, recv_sem, send_sem, local_sem):
    row = lax.axis_index("row")
    col = lax.axis_index("col")
    other = row + 1 - 2 * lax.rem(row, 2)
    level = col // 4
    half = lax.rem(col // 2, 2)
    core = lax.rem(col, 2)
    count, row_len, step = buf.shape[1:]
    features = dens.shape[1]

    src_level, src_half, src_core = block // 4, (block // 2) % 2, block % 2
    here = (src_level, src_half, src_core)

    top_src = col == TOP
    top_recv = level >= UPPER
    from_src = jnp.logical_and(level == UPPER, core == 1)
    top_from_row = jnp.where(jnp.logical_and(from_src, half == 0), other, row)
    top_from_col = jnp.where(core == 0, col + 1, jnp.where(from_src, TOP, col - 4))
    top_up = both(core == 1, level >= UPPER, level < 7)
    top_mate = both(core == 1, level >= UPPER)

    same = block == TOP
    src = col == block
    root_col = src_level * 4 + (1 - src_half) * 2 + src_half
    root = col == root_col
    up_dst = both(level > src_level, level < UPPER)
    relay_zero = jnp.logical_and(src_level == 3, both(level == 0, core == 1))
    root_needs = jnp.logical_and(col > block, level == src_level)
    recv = jnp.logical_or(jnp.logical_or(col > block, root), relay_zero)
    if same:
        recv = col < 0
        src = col < 0
        root = col < 0
    src_dev = jnp.where(half == src_half, block, root_col)
    turn = 6 if src_level == 3 else UPPER
    on_mate = jnp.logical_and(core == 1, col > block)
    if src_level == 3:
        entry_up = both(level == UPPER, core == 0)
        entry_down = both(level == 0, core == 1)
        from_zero = both(level == 7, core == 0)
    else:
        entry_up = both(level == src_level + 1, core == 0)
        entry_down = both(level == 7, core == 0)
        from_zero = col < 0
    from_col = jnp.where(
        root,
        block,
        jnp.where(
            on_mate,
            col - 1,
            jnp.where(
                jnp.logical_or(entry_up, entry_down),
                src_dev,
                jnp.where(from_zero, half * 2 + 1, jnp.where(level >= turn, col + 4, col - 4)),
            ),
        ),
    )
    from_row = jnp.where(root, other, row)
    start = jnp.logical_or(src, root)
    down_entry_col = (1 if src_level == 3 else 28) + half * 2
    none = col < 0
    if same:
        sends = []
        root_send = none
    else:
        up_relay = both(core == 0, level > src_level, level < turn - 1)
        up = jnp.logical_or(start, up_relay)
        up_col = jnp.where(start, (src_level + 1) * 4 + half * 2, col + 4)
        down_relay = both(core == 0, level > turn)
        zero_relay = both(core == 1, level == 0) if src_level == 3 else none
        down = jnp.logical_or(jnp.logical_or(start, down_relay), zero_relay)
        down_col = jnp.where(start, down_entry_col, jnp.where(zero_relay, 28 + half * 2, col - 4))
        mate = jnp.logical_and(core == 0, col >= block)
        sends = [(up, up_col), (down, down_col), (mate, col + 1)]
        root_send = src

    barrier = pltpu.get_barrier_semaphore()

    @pl.when(top_recv)
    def _():
        pl.semaphore_signal(barrier, 1, device_id=(top_from_row, top_from_col), device_id_type=MESH_ID)

    @pl.when(recv)
    def _():
        pl.semaphore_signal(barrier, 1, device_id=(from_row, from_col), device_id_type=MESH_ID)

    one = lambda cond: jnp.where(cond, 1, 0)
    total = 2 * one(top_src) + one(top_up) + one(top_mate) + one(root_send)
    for cond, _ in sends:
        total = total + one(cond)

    def copy(which, slot, j, src_ref, to_row, to_col):
        return pltpu.make_async_remote_copy(
            src_ref=src_ref,
            dst_ref=buf.at[which, j],
            send_sem=send_sem.at[which, slot, j],
            recv_sem=recv_sem.at[which, j],
            device_id=(to_row, to_col),
            device_id_type=MESH_ID,
        )

    def held(which, j):
        return buf.at[which, j]

    def each(body):
        def step_of(j, carry):
            body(j)
            return carry

        lax.fori_loop(0, count, step_of, 0)

    any_src = jnp.logical_or(top_src, src)

    def load(k, r):
        rows = dens.at[pl.ds(pl.multiple_of(r * row_len, 8), row_len)]
        return pltpu.make_async_copy(rows, rows_in.at[k], local_sem.at[k])

    @pl.when(any_src)
    def _():
        load(0, row).start()
        load(1, other).start()
        load(0, row).wait()
        load(1, other).wait()
        for k in range(2):
            for j in range(count):
                width = min(step, features - j * step)
                pieces[k, j, :, 0:width] = rows_in[k, :, j * step : j * step + width]

    @pl.when(total > 0)
    def _():
        pl.semaphore_wait(barrier, total)

    @pl.when(top_src)
    def _():
        def send(j):
            copy(0, 0, j, pieces.at[0, j], row, UPPER * 4 + 3).start()
            copy(0, 1, j, pieces.at[1, j], other, UPPER * 4 + 1).start()

        each(send)

    if not same:

        @pl.when(src)
        def _():
            def send(j):
                copy(1, 3, j, pieces.at[1, j], other, root_col).start()
                for slot, (cond, to_col) in enumerate(sends):

                    @pl.when(cond)
                    def _():
                        copy(1, slot, j, pieces.at[0, j], row, to_col).start()

            each(send)

    if not same:

        @pl.when(jnp.logical_and(recv, jnp.logical_not(on_mate)))
        def _():
            def pass_on(j):
                copy(1, 0, j, held(1, j), row, col).wait_recv()
                for slot, (cond, to_col) in enumerate(sends):

                    @pl.when(cond)
                    def _():
                        copy(1, slot, j, held(1, j), row, to_col).start()

            each(pass_on)

    @pl.when(top_mate)
    def _():
        def pass_on(j):
            copy(0, 0, j, held(0, j), row, col).wait_recv()

            @pl.when(top_up)
            def _():
                copy(0, 1, j, held(0, j), row, col + 4).start()

            copy(0, 0, j, held(0, j), row, col - 1).start()

        each(pass_on)

    @pl.when(both(top_recv, core == 0))
    def _():
        each(lambda j: copy(0, 0, j, held(0, j), row, col).wait_recv())

    if not same:

        @pl.when(on_mate)
        def _():
            each(lambda j: copy(1, 0, j, held(1, j), row, col).wait_recv())

    def write(which, ref):
        return pltpu.make_async_copy(ref, out.at[which], local_sem.at[2 + which])

    for which, mine in ((0, top_src), (1, src)):

        @pl.when(mine)
        def _():
            write(which, pieces.at[0]).start()

        @pl.when(jnp.logical_not(mine))
        def _():
            write(which, buf.at[which]).start()

    @pl.when(top_src)
    def _():
        def wait(j):
            copy(0, 0, j, held(0, j), row, col).wait_send()
            copy(0, 1, j, held(0, j), row, col).wait_send()

        each(wait)

    @pl.when(top_mate)
    def _():
        each(lambda j: copy(0, 0, j, held(0, j), row, col).wait_send())

    @pl.when(top_up)
    def _():
        each(lambda j: copy(0, 1, j, held(0, j), row, col).wait_send())

    for slot, (cond, _) in enumerate(sends):

        @pl.when(cond)
        def _():
            each(lambda j: copy(1, slot, j, held(1, j), row, col).wait_send())

    if not same:

        @pl.when(src)
        def _():
            each(lambda j: copy(1, 3, j, held(1, j), row, col).wait_send())

    for which in range(2):
        write(which, buf.at[which]).wait()


def spread(block, row_len, dens):
    features = dens.shape[1]
    count = -(-features // STEP)
    return pl.pallas_call(
        functools.partial(spread_kernel, block),
        name=f"spread_{block}",
        out_shape=jax.ShapeDtypeStruct((2, count, row_len, STEP), dens.dtype),
        in_specs=[pl.BlockSpec(memory_space=pl.ANY)],
        out_specs=pl.BlockSpec(memory_space=pl.ANY),
        scratch_shapes=[
            pltpu.VMEM((2, count, row_len, STEP), dens.dtype),
            pltpu.VMEM((2, row_len, features), dens.dtype),
            pltpu.VMEM((2, count, row_len, STEP), dens.dtype),
            pltpu.SemaphoreType.DMA((2, count)),
            pltpu.SemaphoreType.DMA((2, 4, count)),
            pltpu.SemaphoreType.DMA((4,)),
        ],
        compiler_params=pltpu.CompilerParams(
            collective_id=block, has_side_effects=True, vmem_limit_bytes=8 * 1024 * 1024
        ),
    )(dens)


def split3(x):
    hi = x.astype(jnp.bfloat16)
    rest = x - hi.astype(jnp.float32)
    mid = rest.astype(jnp.bfloat16)
    low = (rest - mid.astype(jnp.float32)).astype(jnp.bfloat16)
    return hi, mid, low


def dot_t(a, b):
    return lax.dot_general(a, b, (((1,), (1,)), ((), ())), preferred_element_type=jnp.float32)


def pick(table, index):
    states = table.shape[1]
    hit = lax.broadcasted_iota(jnp.int32, (states, index.shape[1]), 0) == index
    hit = jnp.where(hit, 1.0, 0.0).astype(jnp.bfloat16)
    parts = jnp.dot(table, hit, preferred_element_type=jnp.float32)
    u = parts[0:1] + parts[1:2] + parts[2:3]
    v = parts[3:4] + parts[4:5] + parts[5:6]
    return u, v


def prepare_kernel(blocks, _, strength, energies, qp, label, amp_u, amp_v, col_out, row_out, win_f, win_i, near_f, near_i, sem):
    row = lax.axis_index("row")
    col = lax.axis_index("col")
    block_len = col_out.shape[1]
    row_len = row_out.shape[1]
    f32 = jnp.float32
    odd = lax.rem(col, 2)
    base = pl.multiple_of(col * block_len - 64 * odd, 128)
    moving = blocks[0] + blocks[1] - TOP
    firsts = [TOP * block_len + row * row_len, moving * block_len + row * row_len]
    nears = [pl.multiple_of(first // 128 * 128, 128) for first in firsts]
    copies = []
    wide = pl.ds(base, block_len + 64)
    for i, (src, dst) in enumerate(
        [
            (strength.at[:, wide], win_f),
            (qp.at[:, wide], win_i.at[pl.ds(0, 2)]),
            (label.at[:, wide], win_i.at[pl.ds(2, 1)]),
        ]
        + [
            pair
            for k in range(2)
            for pair in (
                (strength.at[:, pl.ds(nears[k], 256)], near_f.at[k, pl.ds(0, 1)]),
                (energies.at[:, pl.ds(nears[k], 256)], near_f.at[k, pl.ds(1, 1)]),
                (qp.at[:, pl.ds(nears[k], 256)], near_i.at[k, pl.ds(0, 2)]),
                (label.at[:, pl.ds(nears[k], 256)], near_i.at[k, pl.ds(2, 1)]),
            )
        ]
    ):
        copies.append(pltpu.make_async_copy(src, dst, sem.at[i]))
        copies[-1].start()
    table = jnp.concatenate(
        [t.astype(f32) for t in (*split3(amp_u[...]), *split3(amp_v[...]))] + [jnp.zeros((2, amp_u.shape[1]), f32)], 0
    ).astype(jnp.bfloat16)

    def factors(pairs):
        u_i, v_i = pick(table, pairs[0:1])
        u_j, v_j = pick(table, pairs[1:2])
        return u_i * v_j + v_i * u_j, u_i * u_j - v_i * v_j

    for copy in copies:
        copy.wait()

    def own(x):
        return jnp.where(odd == 1, x[:, 64:], x[:, :block_len])

    whole = own(win_i[...])
    anomal, direct = factors(whole[0:2])
    col_out[0:1, :] = anomal
    col_out[1:2, :] = direct
    col_out[2:3, :] = whole[2:3].astype(f32)
    col_out[3:4, :] = own(win_f[...])
    for k in range(2):
        block = (TOP, moving)[k]
        shift = firsts[k] - nears[k]
        ints = pltpu.roll(near_i[k], 256 - shift, axis=1)[:, :128]
        floats = pltpu.roll(near_f[k], 256 - shift, axis=1)[:, :128]
        anomal, direct = factors(ints[0:2])
        lane = lax.broadcasted_iota(jnp.int32, (1, 128), 1)
        diagonal = firsts[k] + lane - col * block_len
        packed = jnp.concatenate(
            [
                anomal,
                direct,
                ints[2:3].astype(f32),
                floats[1:2],
                floats[0:1],
                diagonal.astype(f32),
                jnp.full((1, 128), jnp.where(col >= block, 1.0, 0.0), f32),
                jnp.full((1, 128), jnp.where(blocks[k] == TOP, 1.0, 0.0), f32),
            ],
            0,
        )
        row_out[k] = jnp.concatenate([packed, jnp.zeros((120, 128), f32)], 0).T[:row_len]


def prepare(block_len, row_len, blocks, panels, strength, energies, qp, label, amp_u, amp_v):
    anywhere = pl.BlockSpec(memory_space=pl.ANY)
    vmem = pl.BlockSpec(memory_space=pltpu.VMEM)
    out = jax.ShapeDtypeStruct
    return pl.pallas_call(
        prepare_kernel,
        name="prepare",
        out_shape=(out((8, block_len), jnp.float32), out((2, row_len, 128), jnp.float32)),
        in_specs=[pl.BlockSpec(memory_space=pltpu.SMEM)] + [anywhere] * 5 + [vmem] * 2,
        out_specs=(vmem, vmem),
        scratch_shapes=[
            pltpu.VMEM((1, block_len + 64), jnp.float32),
            pltpu.VMEM((4, block_len + 64), jnp.int32),
            pltpu.VMEM((2, 8, 256), jnp.float32),
            pltpu.VMEM((2, 8, 256), jnp.int32),
            pltpu.SemaphoreType.DMA((11,)),
        ],
        compiler_params=pltpu.CompilerParams(vmem_limit_bytes=16 * 1024 * 1024),
    )(blocks, panels, strength, energies, qp, label, amp_u, amp_v)


def finish_kernel(
    panels,
    dens,
    coup_a,
    coup_b,
    col_in,
    row_in,
    mat_a,
    mat_b,
    response,
    mirror,
    weight,
    weighted,
    dens_v,
    dens_sem,
    acc,
    resp_all,
    mir_pair,
    mir_all,
    resp_send,
    resp_recv,
    pair_send,
    pair_recv,
    mir_send,
    mir_recv,
):
    row = lax.axis_index("row")
    col = lax.axis_index("col")
    rows = lax.axis_size("row")
    cols = lax.axis_size("col")
    other = row + 1 - 2 * lax.rem(row, 2)
    deep = rows // 2
    z = row // 2
    row_len = mat_a.shape[1]
    block_len = dens.shape[0]
    features = dens.shape[1]
    total = block_len * cols

    barrier = pltpu.get_barrier_semaphore()

    def greet_col(d, _):
        pl.semaphore_signal(barrier, 1, device_id=(row, lax.rem(col + d, cols)), device_id_type=MESH_ID)
        return 0

    def greet_deep(d, _):
        to = lax.rem(z + d, deep) * 2 + lax.rem(row, 2)
        pl.semaphore_signal(barrier, 1, device_id=(to, col), device_id_type=MESH_ID)
        return 0

    lax.fori_loop(1, cols, greet_col, 0)
    lax.fori_loop(1, deep, greet_deep, 0)
    pl.semaphore_signal(barrier, 1, device_id=(other, col), device_id_type=MESH_ID)

    tile = dens_v.shape[0] // 4 // 128 * 128 + 128
    parts = [(lo, min(tile, block_len - lo)) for lo in range(0, block_len, tile)]

    def fetch(i):
        at = pl.ds(*parts[i])
        return pltpu.make_async_copy(dens.at[at], dens_v.at[at], dens_sem.at[i])

    for i in range(len(parts)):
        fetch(i).start()

    types, points = coup_a.shape
    for t in range(types):
        weight[0:1, t * points : (t + 1) * points] = coup_a[t : t + 1, :]
        weight[1:2, t * points : (t + 1) * points] = coup_b[t : t + 1, :]

    spans = [(lo, min(STEP, features - lo)) for lo in range(0, features, STEP)]
    for j, (lo, size) in enumerate(spans):
        at = pl.ds(lo, size)
        wa = weight[0:1, at]
        wb = weight[1:2, at]
        stack = []
        for k in range(2):
            p = panels[k, j, :, :size].astype(jnp.float32)
            stack += [p * wa, p * wb]
        weighted[:, at] = jnp.concatenate(stack, 0).astype(jnp.bfloat16)

    for i, (first, size) in enumerate(parts):
        fetch(i).wait()
        acc[:, first : first + size] = dot_t(weighted[...], dens_v[first : first + size, :])

    col_anomal = col_in[0:1, :]
    col_direct = col_in[1:2, :]
    col_label = col_in[2:3, :]
    col_strength = col_in[3:4, :]
    lane = lax.broadcasted_iota(jnp.int32, (1, block_len), 1).astype(jnp.float32)
    mats = []
    for k in range(2):
        anomal, direct, lab, energy, stren, diagonal, active, _ = (row_in[k, :, i : i + 1] for i in range(8))
        agree = lab == col_label
        prod_a = acc[2 * k * row_len : (2 * k + 1) * row_len]
        prod_b = acc[(2 * k + 1) * row_len : (2 * k + 2) * row_len]
        a = prod_a + jnp.where(diagonal == lane, energy, 0.0)
        a = a + PAIRING * jnp.where(agree, anomal * col_anomal, 0.0)
        b = prod_b + PAIRING * jnp.where(agree, direct * col_direct, 0.0)
        a = jnp.where(active > 0.0, a, 0.0)
        b = jnp.where(active > 0.0, b, 0.0)
        both_ab = a + b
        down = jnp.sum(both_ab * stren, axis=0, keepdims=True)
        across = jnp.sum(both_ab * col_strength, axis=1, keepdims=True)
        mats.append((a, b, down, across))
    resp = []
    for k in range(2):
        is_top = row_in[k, :, 7:8] > 0.0
        mat_a[k] = jnp.where(is_top, mats[0][0], mats[1][0])
        mat_b[k] = jnp.where(is_top, mats[0][1], mats[1][1])
        mir_pair[0, k : k + 1, :] = jnp.where(is_top[0:1], mats[0][2], mats[1][2])
        resp.append(jnp.where(is_top, mats[0][3], mats[1][3]))
    wide_resp = jnp.concatenate(resp + [jnp.zeros((128 - 2 * row_len, 1), jnp.float32)], 0)
    resp_all[col] = jnp.broadcast_to(wide_resp, (128, 128)).T[0:1]

    pl.semaphore_wait(barrier, cols - 1 + deep - 1 + 1)

    def send_resp(d, _):
        pltpu.make_async_remote_copy(
            src_ref=resp_all.at[col],
            dst_ref=resp_all.at[col],
            send_sem=resp_send,
            recv_sem=resp_recv,
            device_id=(row, lax.rem(col + d, cols)),
            device_id_type=MESH_ID,
        ).start()
        return 0

    pair = pltpu.make_async_remote_copy(
        src_ref=mir_pair.at[0],
        dst_ref=mir_pair.at[1],
        send_sem=pair_send,
        recv_sem=pair_recv,
        device_id=(other, col),
        device_id_type=MESH_ID,
    )
    pair.start()
    lax.fori_loop(1, cols, send_resp, 0)
    pair.wait_recv()
    mir_all[z] = (mir_pair[0] + mir_pair[1]).astype(mir_all.dtype)

    def send_mir(d, _):
        to = lax.rem(z + d, deep) * 2 + lax.rem(row, 2)
        pltpu.make_async_remote_copy(
            src_ref=mir_all.at[z],
            dst_ref=mir_all.at[z],
            send_sem=mir_send,
            recv_sem=mir_recv,
            device_id=(to, col),
            device_id_type=MESH_ID,
        ).start()
        return 0

    lax.fori_loop(1, deep, send_mir, 0)

    def wait_all(ref, count, sem):
        some = ref.at[pl.ds(0, count)]
        pltpu.make_async_copy(some, some, sem).wait()

    wait_all(resp_all, cols - 1, resp_recv)
    r = jnp.sum(resp_all[...], axis=0) * (1.0 / math.sqrt(total))
    response[0:1, :] = r[:, :row_len]
    response[1:2, :] = r[:, row_len : 2 * row_len]
    wait_all(mir_all, deep - 1, mir_recv)
    m = jnp.sum(mir_all[...].astype(jnp.float32), axis=0) * (1.0 / math.sqrt(block_len))
    mirror[...] = m
    wait_all(resp_all, cols - 1, resp_send)
    wait_all(mir_all, deep - 1, mir_send)
    pair.wait_send()


def finish(rows, cols, panels, dens, coup_a, coup_b, col_in, row_in):
    row_len = panels.shape[2]
    block_len, features = dens.shape
    vmem = pl.BlockSpec(memory_space=pltpu.VMEM)
    out = jax.ShapeDtypeStruct
    f32 = jnp.float32
    return pl.pallas_call(
        finish_kernel,
        name="finish",
        out_shape=(
            out((2, row_len, block_len), f32),
            out((2, row_len, block_len), f32),
            out((2, row_len), f32),
            out((2, block_len), f32),
        ),
        in_specs=[vmem, pl.BlockSpec(memory_space=pl.ANY)] + [vmem] * 4,
        out_specs=(vmem,) * 4,
        scratch_shapes=[
            pltpu.VMEM((8, features), f32),
            pltpu.VMEM((4 * row_len, features), dens.dtype),
            pltpu.VMEM((block_len, features), dens.dtype),
            pltpu.SemaphoreType.DMA((4,)),
            pltpu.VMEM((4 * row_len, block_len), f32),
            pltpu.VMEM((cols, 1, 128), f32),
            pltpu.VMEM((2, 2, block_len), f32),
            pltpu.VMEM((rows // 2, 2, block_len), jnp.bfloat16),
        ]
        + [pltpu.SemaphoreType.DMA] * 6,
        compiler_params=pltpu.CompilerParams(
            collective_id=TOP + 1, has_side_effects=True, vmem_limit_bytes=36 * 1024 * 1024
        ),
    )(panels, dens, coup_a, coup_b, col_in, row_in)


def on_device(
    densities, coupling_a, coupling_b, energies, strength, qp_index, kpi_label, amplitude_u, amplitude_v, panel_blocks
):
    rows = lax.axis_size("row")
    cols = lax.axis_size("col")
    block_len = densities.shape[0]
    row_len = block_len // rows
    flat = lambda x: x.reshape(1, -1)
    moving = panel_blocks[0] + panel_blocks[1] - TOP
    branches = [functools.partial(spread, block, row_len) for block in range(TOP + 1)]
    panels = lax.switch(moving, branches, densities)
    col_in, row_in = prepare(
        block_len,
        row_len,
        panel_blocks,
        panels,
        flat(strength),
        flat(energies),
        qp_index.T,
        flat(kpi_label),
        flat(amplitude_u),
        flat(amplitude_v),
    )
    return finish(rows, cols, panels, densities, coupling_a, coupling_b, col_in, row_in)


def solution(mesh):
    placed = (P("col", None), P(), P(), P(), P(), P(), P(), P(), P(), P())
    return jax.shard_map(
        on_device,
        mesh=mesh,
        in_specs=placed,
        out_specs=(P(None, "row", "col"), P(None, "row", "col"), P(None, "row"), P(None, "col")),
        check_vma=False,
    )
```
